32 devices in a mesh: groups: 2 (over x), tm: 16 (over z, y, core).
Axes of the slice: x: 2, y: 2, z: 4, core: 2. Of those that a mesh axis runs over, the one named last changes fastest.
Arguments:
- queries: bfloat16 [12288, 2240], P(('groups', 'tm')), parts along dimension 0, may hold values from -40 to 40
- keys: bfloat16 [12288, 2240], P(('groups', 'tm')), parts along dimension 0, may hold values from -6 to 6
- values: bfloat16 [12288, 2240], P(('groups', 'tm')), parts along dimension 0, may hold values from -6 to 6
- cross_queries: bfloat16 [12288, 2240], P(('groups', 'tm')), parts along dimension 0, may hold values from -540 to 540
- prompt_keys: bfloat16 [32, 128, 2240], P(('groups', 'tm')), parts along dimension 0, may hold values from -6 to 6
- prompt_values: bfloat16 [32, 128, 2240], P(('groups', 'tm')), parts along dimension 0, may hold values from -6 to 6
- caption_keys: bfloat16 [256, 2240], P('groups'), parts along dimension 0, may hold values from -6 to 6
- caption_values: bfloat16 [256, 2240], P('groups'), parts along dimension 0, may hold values from -6 to 6
- span_start: int32 [32], P('groups'), parts along dimension 0, may hold values from 0 to 15, as said below
- span_end: int32 [32], P('groups'), parts along dimension 0, may hold values from 1 to 16
- prompt_tokens: int32 [32], P('groups'), parts along dimension 0, may hold values from 80 to 128, as said below
- region_mask: int32 [32, 3], P('groups'), parts along dimension 0, may hold values 0 or 1
- out_gain: float32 [2240], replicated, may hold values from 0.5 to 1.5
Outputs:
- self_mixed: bfloat16 [12288, 2240], P(('groups', 'tm')), parts along dimension 0
- cross_mixed: bfloat16 [12288, 2240], P(('groups', 'tm')), parts along dimension 0
The draws below stay inside these ranges and needn't reach their ends.
There are 2 independent parts, one for each index of `groups`. The reference program is written for one: setup_inputs(seed, part) draws one part's arguments, and reference() takes and returns one part's arrays. A program takes and returns all parts, laid end to end along the dimension named above; an argument that names none is the same for every part. Nothing has to cross between parts.
Inputs may be any that keep to these rules, and one draw needn't show every extreme that they name: Prompt p applies to stretches span_start[p] to span_end[p] - 1, with p <= span_start[p] <= p + 1 and span_start[p] < span_end[p] <= p + 6; prompt 0 covers stretches 0 to 5. `prompt_tokens`: prompt 0 uses all 128 slots.
All inputs are finite; a program needn't handle non-finite values.
Results may differ from the reference program's by a relative error of at most 0.007.
Values may be sent and summed in bfloat16 or wider, within the bound.
A program may use at most 128 MiB of HBM per device.

```python
import math
import jax
import jax.numpy as jnp
from jax import lax

D = 2240
HD = 32
TOK_DEV = 384
TILES = 3
STRETCHES = 16
TOKENS = 6144
SPAN = 6
PR_DEV = 1
PROMPTS = 16
PL = 128
GL = 128


def caption_base(key):
    return jnp.clip(jax.random.normal(jax.random.fold_in(key, 11), (GL, D), jnp.float32), -6.0, 6.0)


def draw_caption_keys(key, part):
    drawn = caption_base(key)
    return drawn.astype(jnp.bfloat16)


def draw_cross_queries(key, part):
    drawn = jnp.clip(jax.random.normal(jax.random.fold_in(key, 21), (TOKENS, D), jnp.float32), -6.0, 6.0)
    return drawn.astype(jnp.bfloat16)


def draw_queries(key, part):
    head_count = D // HD
    head_scale = jnp.exp(jax.random.uniform(jax.random.fold_in(key, 31), (head_count,), jnp.float32, 0.0, math.log(10.0)))
    drawn = jnp.clip(jax.random.normal(jax.random.fold_in(key, 33), (TOKENS, D), jnp.float32), -4.0, 4.0)
    column_scale = jnp.repeat(head_scale, HD)
    return (drawn * column_scale[None, :]).astype(jnp.bfloat16)


def span_pair(key):
    prompt_ids = jnp.arange(PROMPTS, dtype=jnp.int32)
    owner_ids = prompt_ids // PR_DEV
    offset = jax.random.randint(jax.random.fold_in(key, 41), (PROMPTS,), 0, 2, dtype=jnp.int32)
    offset = jnp.where(prompt_ids == 0, 0, offset)
    room_left = SPAN - offset
    partial_len = 1 + jax.random.randint(jax.random.fold_in(key, 42), (PROMPTS,), 0, 1 << 20, dtype=jnp.int32) % room_left
    full_reach = jax.random.randint(jax.random.fold_in(key, 43), (PROMPTS,), 0, 10, dtype=jnp.int32) < 7
    length = jnp.where(full_reach, room_left, partial_len)
    length = jnp.where(prompt_ids == 0, SPAN, length)
    begins = jnp.minimum(owner_ids + offset, STRETCHES - 1)
    finish = jnp.minimum(begins + length, STRETCHES)
    return (begins.astype(jnp.int32), finish.astype(jnp.int32))


def draw_span_start(key, part):
    return span_pair(key)[0]


def draw_span_end(key, part):
    return span_pair(key)[1]


def draw_prompt_tokens(key, part):
    least = PL * 5 // 8
    counts = jax.random.randint(jax.random.fold_in(key, 51), (PROMPTS,), least, PL + 1, dtype=jnp.int32)
    prompt_ids = jnp.arange(PROMPTS)
    counts = jnp.where(prompt_ids == 1, least, counts)
    return jnp.where(prompt_ids == 0, PL, counts).astype(jnp.int32)


def with_ends(result, key, low, high):
    dims = result.shape
    spot = [jax.random.randint(jax.random.fold_in(key, axis), (), 0, dims[axis]) for axis in range(len(dims))]
    result = result.at[tuple(spot)].set(low)
    longest = dims.index(max(dims))
    spot[longest] = (spot[longest] + 1) % dims[longest]
    return result.at[tuple(spot)].set(high)


def level_of(rng, extent, pieces, low, top_value):
    def one(position, shards_of):
        heights = jax.random.uniform(jax.random.fold_in(jax.random.fold_in(rng, 6), position), (shards_of,), jnp.float32, low / len(pieces), top_value / len(pieces))
        return jnp.repeat(jnp.exp(heights), extent[position] // shards_of).reshape((-1,) + (1,) * (len(extent) - position - 1))

    loudness = one(*pieces[0])
    for cut in pieces[1:]:
        loudness = loudness * one(*cut)
    return loudness


def scatter_about(own_key, extent, scale, bound, shards=(), kind=jnp.bfloat16):
    loudness = level_of(own_key, extent, shards, -0.22, 0.18) if shards else 1.0
    values = jax.random.normal(own_key, extent, jnp.float32) * scale * loudness
    return jnp.minimum(jnp.maximum(values, -bound), bound).astype(kind)


def setup_inputs(seed: int = 0, part: int = 0) -> dict:
    splits = jax.random.split(jax.random.key(seed), 14)
    own_keys = jax.random.split(jax.random.fold_in(splits[13], part), 14)
    return {
        "queries": draw_queries(jax.random.fold_in(jax.random.fold_in(splits[13], part), 71), part),
        "keys": scatter_about(own_keys[1], (TOKENS, D), 1.0, 6.0, ((0, 16),)),
        "values": scatter_about(own_keys[2], (TOKENS, D), 1.0, 6.0, ((0, 16),)),
        "cross_queries": draw_cross_queries(jax.random.fold_in(jax.random.fold_in(splits[13], part), 71), part),
        "prompt_keys": scatter_about(own_keys[4], (PROMPTS, PL, D), 1.0, 6.0, ((0, 16),)),
        "prompt_values": scatter_about(own_keys[5], (PROMPTS, PL, D), 1.0, 6.0, ((0, 16),)),
        "caption_keys": draw_caption_keys(jax.random.fold_in(jax.random.fold_in(splits[13], part), 71), part),
        "caption_values": scatter_about(own_keys[7], (GL, D), 1.0, 6.0),
        "span_start": draw_span_start(jax.random.fold_in(jax.random.fold_in(splits[13], part), 71), part),
        "span_end": draw_span_end(jax.random.fold_in(jax.random.fold_in(splits[13], part), 71), part),
        "prompt_tokens": draw_prompt_tokens(jax.random.fold_in(jax.random.fold_in(splits[13], part), 71), part),
        "region_mask": with_ends((jax.random.randint(own_keys[11], (PROMPTS, TILES), 0, 2) < 1).astype(jnp.int32), jax.random.fold_in(own_keys[11], 1), 0, 1),
        "out_gain": jnp.clip(1.0 + 0.1 * jax.random.normal(splits[12], (D,), jnp.float32), 0.5, 1.5),
    }


def prompt_tiles(owner_id, stretch_id, span_start, span_end, prompt_tokens, region_mask):
    first_row = jnp.maximum(owner_id, 0).astype(jnp.int32) * PR_DEV
    begins = lax.dynamic_slice_in_dim(span_start, first_row, PR_DEV, 0)
    finish = lax.dynamic_slice_in_dim(span_end, first_row, PR_DEV, 0)
    counts = lax.dynamic_slice_in_dim(prompt_tokens, first_row, PR_DEV, 0)
    regions = lax.dynamic_slice_in_dim(region_mask, first_row, PR_DEV, 0)
    covers = (owner_id >= 0) & (begins <= stretch_id) & (stretch_id < finish)
    live_keys = jnp.arange(PL, dtype=jnp.int32)[None, :] < counts[:, None]
    visible_set = covers[:, None, None] & (regions[:, :, None] == 1) & live_keys[:, None, :]
    return jnp.transpose(visible_set, (1, 0, 2)).reshape(regions.shape[1], PR_DEV * PL)

def per_token(tile_mask, tok_rows):
    tile_count, key_count = tile_mask.shape
    spread_out = jnp.broadcast_to(tile_mask[:, None, :], (tile_count, tok_rows // tile_count, key_count))
    return spread_out.reshape(tok_rows, key_count)

def reference(queries, keys, values, cross_queries, prompt_keys, prompt_values, caption_keys, caption_values, span_start, span_end, prompt_tokens, region_mask, out_gain):
    head_count = D // HD
    lifted_q = jnp.maximum(queries, 0).astype(jnp.float32).reshape(STRETCHES, TOK_DEV, head_count, HD)
    lifted_k = jnp.maximum(keys, 0).astype(jnp.float32).reshape(STRETCHES, TOK_DEV, head_count, HD)
    value_rows = values.astype(jnp.float32).reshape(STRETCHES, TOK_DEV, head_count, HD)
    stretch_state = jnp.einsum('crhd,crhe->chde', lifted_k, value_rows)
    running = jnp.cumsum(stretch_state, axis=0)
    prior_state = jnp.concatenate([jnp.zeros_like(stretch_state[:1]), running[:-1]], axis=0)
    whole_state = (prior_state + stretch_state).astype(jnp.bfloat16)
    whole_state = lax.optimization_barrier(whole_state).astype(jnp.float32)
    raw_mix = jnp.einsum('crhd,chde->crhe', lifted_q, whole_state).reshape(TOKENS, D)
    mean_square = lax.optimization_barrier(jnp.mean(raw_mix * raw_mix, axis=-1, keepdims=True))
    self_mixed = (raw_mix * lax.rsqrt(mean_square + 1e-05) * out_gain[None, :]).astype(jnp.bfloat16)
    caption_k = caption_keys.astype(jnp.float32).reshape(GL, head_count, HD)
    caption_v = caption_values.astype(jnp.float32).reshape(GL, head_count, HD)
    stretch_queries = cross_queries.reshape(STRETCHES, TOK_DEV, head_count, HD)
    score_scale = HD ** (-0.5)

    def one_stretch(packed):
        stretch_id, query_rows = packed
        query_rows = query_rows.astype(jnp.float32)
        owners = stretch_id - jnp.arange(SPAN, dtype=jnp.int32)

        def pick(owner_id):
            first_row = jnp.maximum(owner_id, 0).astype(jnp.int32) * PR_DEV
            picked_k = lax.dynamic_slice_in_dim(prompt_keys, first_row, PR_DEV, 0)
            picked_v = lax.dynamic_slice_in_dim(prompt_values, first_row, PR_DEV, 0)
            tile_mask = prompt_tiles(owner_id, stretch_id, span_start, span_end, prompt_tokens, region_mask)
            return (picked_k, picked_v, tile_mask)
        picked_k, picked_v, tile_masks = jax.vmap(pick)(owners)
        window = SPAN * PR_DEV * PL
        all_keys = jnp.concatenate([caption_k, picked_k.astype(jnp.float32).reshape(window, head_count, HD)], axis=0)
        all_values = jnp.concatenate([caption_v, picked_v.astype(jnp.float32).reshape(window, head_count, HD)], axis=0)
        tile_all = jnp.concatenate([jnp.ones((TILES, GL), dtype=bool), jnp.transpose(tile_masks, (1, 0, 2)).reshape(TILES, window)], axis=1)
        visible = per_token(tile_all, TOK_DEV)
        scores = jnp.einsum('rhd,khd->hrk', query_rows, all_keys) * score_scale
        scores = jnp.where(visible[None], scores, -1e+30)
        peak = lax.optimization_barrier(jnp.max(scores, axis=2))
        expo = jnp.where(visible[None], jnp.exp(scores - peak[:, :, None]), 0.0)
        denom = lax.optimization_barrier(jnp.sum(expo, axis=2))
        weights = lax.optimization_barrier(expo.astype(jnp.bfloat16)).astype(jnp.float32)
        summed = jnp.einsum('hrk,khd->rhd', weights, all_values)
        mixed_rows = summed / jnp.transpose(denom)[:, :, None]
        return mixed_rows.reshape(TOK_DEV, D).astype(jnp.bfloat16)
    cross_mixed = lax.map(one_stretch, (jnp.arange(STRETCHES, dtype=jnp.int32), stretch_queries))
    return (self_mixed, cross_mixed.reshape(TOKENS, D))
```

```python
import functools
import math

import jax
import jax.numpy as jnp
from jax import lax
from jax.experimental import pallas as pl
from jax.experimental.pallas import tpu as pltpu
from jax.sharding import PartitionSpec as P

HD = 32
SPAN = 6
LANES = 128
HEADS = LANES // HD
NEG = -1e30


def state_kernel(k_ref, v_ref, s_ref):
    lifted = jnp.maximum(k_ref[...], 0)
    full = lax.dot_general(
        lifted, v_ref[...], (((0,), (0,)), ((), ())), preferred_element_type=jnp.float32
    )
    lane_head = lax.broadcasted_iota(jnp.int32, (HD, LANES), 1) // HD
    total = jnp.zeros((HD, LANES), jnp.float32)
    for h in range(HEADS):
        total = jnp.where(lane_head == h, full[h * HD : (h + 1) * HD, :], total)
    s_ref[...] = total


def stretch_states(keys, values):
    rows, width = keys.shape
    steps = pl.cdiv(width, LANES)
    spec = pl.BlockSpec((rows, LANES), lambda g: (0, g))
    return pl.pallas_call(
        state_kernel,
        grid=(steps,),
        in_specs=[spec, spec],
        out_specs=pl.BlockSpec((HD, LANES), lambda g: (0, g)),
        out_shape=jax.ShapeDtypeStruct((HD, width), jnp.float32),
    )(keys, values)


def mix_kernel(width, q_ref, own_ref, prior_ref, gain_ref, o_ref, raw_ref):
    steps = pl.cdiv(width, LANES)
    rows = q_ref.shape[0]
    square = jnp.zeros((rows, LANES), jnp.float32)
    for g in range(steps):
        lanes = min(LANES, width - g * LANES)
        part = pl.ds(g * LANES, lanes)
        small = (own_ref[:, part] + prior_ref[:, part]).astype(jnp.bfloat16)
        tall = jnp.concatenate([small] * (lanes // HD), axis=0)
        row_head = lax.broadcasted_iota(jnp.int32, (lanes, lanes), 0) // HD
        lane_head = lax.broadcasted_iota(jnp.int32, (lanes, lanes), 1) // HD
        weights = jnp.where(row_head == lane_head, tall, jnp.zeros_like(tall))
        raw = jnp.dot(
            jnp.maximum(q_ref[:, part], 0), weights, preferred_element_type=jnp.float32
        )
        raw_ref[:, part] = raw
        if lanes == LANES:
            square = square + raw * raw
        else:
            tail = jnp.sum(raw * raw, axis=1, keepdims=True)
    total = jnp.sum(square, axis=1, keepdims=True)
    if width % LANES:
        total = total + tail
    scale = lax.rsqrt(total * (1.0 / width) + 1e-05)
    for g in range(steps):
        part = pl.ds(g * LANES, min(LANES, width - g * LANES))
        o_ref[:, part] = (raw_ref[:, part] * scale * gain_ref[:, part]).astype(o_ref.dtype)


def self_mix(queries, own, prior, gain):
    rows, width = queries.shape
    return pl.pallas_call(
        functools.partial(mix_kernel, width),
        out_shape=jax.ShapeDtypeStruct((rows, width), jnp.bfloat16),
        scratch_shapes=[pltpu.VMEM((rows, width), jnp.float32)],
        compiler_params=pltpu.CompilerParams(vmem_limit_bytes=48 * 1024 * 1024),
    )(queries, own, prior, gain[None, :])


def attend_kernel(
    width, slots, tile_rows, tiles, least,
    seen_ref, list_ref, count_ref,
    q_ref, ck_ref, cv_ref, pk_ref, pv_ref, o_ref, k_buf, v_buf,
):
    g = pl.program_id(0)
    live = width - g * LANES
    lane = lax.broadcasted_iota(jnp.int32, (slots, LANES), 1)
    inside = lane < live
    for b in range(SPAN + 1):
        key_block = ck_ref[...] if b == 0 else pk_ref[b - 1]
        value_block = cv_ref[...] if b == 0 else pv_ref[b - 1]
        k_buf[b] = jnp.where(inside, key_block, jnp.zeros_like(key_block))
        v_buf[b] = value_block.T
    tok_lane = lax.broadcasted_iota(jnp.int32, (tile_rows, LANES), 1) // HD
    factor = HD ** (-0.5) * math.log2(math.e)

    def tile(t, blocks):
        first = pl.multiple_of(t * tile_rows, tile_rows)
        q = q_ref[pl.ds(first, tile_rows), :]
        ids = [0] + [list_ref[t * SPAN + i] for i in range(blocks - 1)]
        counts = [None] + [count_ref[ids[i]] for i in range(1, blocks)]
        outs = []
        for pair in range(HEADS // 2):
            heads = (2 * pair, 2 * pair + 1)
            both = jnp.concatenate(
                [jnp.where(tok_lane == h, q, jnp.zeros_like(q)) for h in heads], axis=0
            )
            scores = []
            peak = None
            for i in range(blocks):
                s = lax.dot_general(
                    k_buf[ids[i]], both, (((1,), (1,)), ((), ())),
                    preferred_element_type=jnp.float32,
                )
                if i:
                    row = lax.broadcasted_iota(jnp.int32, (slots - least, 2 * tile_rows), 0) + least
                    s = jnp.concatenate(
                        [s[:least], jnp.where(row < counts[i], s[least:], NEG)], axis=0
                    )
                top = jnp.max(s.reshape(slots // 8, 8, 2 * tile_rows), axis=0)
                peak = top if peak is None else jnp.maximum(peak, top)
                scores.append(s)
            peak = jnp.max(peak, axis=0, keepdims=True)
            denom = None
            acc = None
            for i in range(blocks):
                e = jnp.exp2((scores[i] - peak) * factor)
                part = jnp.sum(e.reshape(slots // 8, 8, 2 * tile_rows), axis=0)
                denom = part if denom is None else denom + part
                added = jnp.dot(
                    v_buf[ids[i], pl.ds(pair * 2 * HD, 2 * HD), :], e.astype(jnp.bfloat16),
                    preferred_element_type=jnp.float32,
                )
                acc = added if acc is None else acc + added
            inverse = 1.0 / jnp.sum(denom, axis=0, keepdims=True)
            outs.append(acc[:HD, :tile_rows] * inverse[:, :tile_rows])
            outs.append(acc[HD:, tile_rows:] * inverse[:, tile_rows:])
        mixed = jnp.concatenate(outs, axis=0)
        o_ref[pl.ds(first, tile_rows), :] = mixed.T.astype(o_ref.dtype)

    @pl.loop(0, tiles)
    def _(t):
        for blocks in range(1, SPAN + 2):
            @pl.when(seen_ref[t] == blocks - 1)
            def _():
                tile(t, blocks)


def cross_mix(queries, caption_keys, caption_values, near_keys, near_values, seen, order, counts):
    rows, width = queries.shape
    slots = caption_keys.shape[0]
    tiles = seen.shape[0]
    steps = pl.cdiv(width, LANES)
    token = pl.BlockSpec((rows, LANES), lambda g, *_: (0, g))
    caption = pl.BlockSpec((slots, LANES), lambda g, *_: (0, g))
    near = pl.BlockSpec((SPAN, slots, LANES), lambda g, *_: (0, 0, g))
    return pl.pallas_call(
        functools.partial(attend_kernel, width, slots, rows // tiles, tiles, slots * 5 // 8),
        grid_spec=pltpu.PrefetchScalarGridSpec(
            num_scalar_prefetch=3,
            grid=(steps,),
            in_specs=[token, caption, caption, near, near],
            out_specs=token,
            scratch_shapes=[
                pltpu.VMEM((SPAN + 1, slots, LANES), jnp.bfloat16),
                pltpu.VMEM((SPAN + 1, LANES, slots), jnp.bfloat16),
            ],
        ),
        out_shape=jax.ShapeDtypeStruct((rows, width), jnp.bfloat16),
        compiler_params=pltpu.CompilerParams(vmem_limit_bytes=48 * 1024 * 1024),
    )(seen, order, counts, queries, caption_keys, caption_values, near_keys, near_values)


def tables(stretch, span_start, span_end, prompt_tokens, region_mask):
    reach = jnp.arange(SPAN, dtype=jnp.int32)
    owner = stretch - reach
    row = jnp.maximum(owner, 0)
    covers = (owner >= 0) & (span_start[row] <= stretch) & (stretch < span_end[row])
    flags = (covers[:, None] & (region_mask[row] == 1)).T.astype(jnp.int32)
    seen = jnp.sum(flags, axis=1)
    place = jnp.cumsum(flags, axis=1) - 1
    hit = (place[:, :, None] == reach[None, None, :]) & (flags[:, :, None] == 1)
    order = jnp.sum(jnp.where(hit, reach[None, :, None] + 1, 0), axis=1)
    counts = jnp.concatenate([jnp.zeros((1,), jnp.int32), prompt_tokens[row]])
    return seen, order.reshape(-1), counts


def local(
    queries, keys, values, cross_queries, prompt_keys, prompt_values, caption_keys,
    caption_values, span_start, span_end, prompt_tokens, region_mask, out_gain,
):
    stretch = lax.axis_index("tm")
    devices = lax.axis_size("tm")
    own = stretch_states(keys, values)
    gathered = lax.all_gather(own.astype(jnp.bfloat16), "tm")
    earlier = jnp.arange(devices) < stretch
    prior = jnp.sum(
        jnp.where(earlier[:, None, None], gathered.astype(jnp.float32), 0.0), axis=0
    )
    self_mixed = self_mix(queries, own, prior, out_gain)
    route = [(i - 1, i) for i in range(1, devices)]
    moving = (prompt_keys, prompt_values)
    blocks = [moving]
    for _ in range(1, SPAN):
        moving = lax.ppermute(moving, "tm", route)
        blocks.append(moving)
    near_keys = jnp.concatenate([b[0] for b in blocks], axis=0)
    near_values = jnp.concatenate([b[1] for b in blocks], axis=0)
    seen, order, counts = tables(stretch, span_start, span_end, prompt_tokens, region_mask)
    cross_mixed = cross_mix(
        cross_queries, caption_keys, caption_values, near_keys, near_values, seen, order, counts
    )
    return (self_mixed, cross_mixed)


def solution(mesh):
    rows = P(("groups", "tm"), None)
    blocks = P(("groups", "tm"), None, None)
    in_specs = (
        rows, rows, rows, rows, blocks, blocks, P("groups", None), P("groups", None),
        P("groups"), P("groups"), P("groups"), P("groups", None), P(),
    )
    return jax.shard_map(
        local, mesh=mesh, in_specs=in_specs, out_specs=(rows, rows), check_vma=False
    )
```

```python
import functools
import math

import jax
import jax.numpy as jnp
from jax import lax
from jax.experimental import pallas as pl
from jax.experimental.pallas import tpu as pltpu
from jax.sharding import PartitionSpec as P

HD = 32
SPAN = 6
PAIR = 2 * HD
NEG = -1e30
VMEM_BYTES = 56 * 1024 * 1024


def head_groups(width):
    heads = width // HD
    return next(heads // n for n in (10, 14, 8, 6, 4, 2) if heads % n == 0)


def state_kernel(k_ref, v_ref, s_ref):
    size = k_ref.shape[0]
    full = lax.dot_general(
        v_ref[...], jnp.maximum(k_ref[...], 0), (((1,), (1,)), ((), ())),
        preferred_element_type=jnp.float32,
    )
    lane_head = lax.broadcasted_iota(jnp.int32, (HD, size), 1) // HD
    total = full[:HD, :]
    for h in range(1, size // HD):
        total = jnp.where(lane_head == h, full[h * HD : (h + 1) * HD, :], total)
    s_ref[0] = total


def stretch_states(keys, values):
    width, rows = keys.shape
    steps = head_groups(width)
    size = width // steps
    spec = pl.BlockSpec((size, rows), lambda g: (g, 0))
    return pl.pallas_call(
        state_kernel,
        grid=(steps,),
        in_specs=[spec, spec],
        out_specs=pl.BlockSpec((1, HD, size), lambda g: (g, 0, 0)),
        out_shape=jax.ShapeDtypeStruct((steps, HD, size), jnp.float32),
    )(keys, values)


def mix_kernel(q_ref, own_ref, prior_ref, gain_ref, o_ref, raw_ref):
    steps, _, size = own_ref.shape
    rows = q_ref.shape[1]
    width = steps * size
    row_head = lax.broadcasted_iota(jnp.int32, (size, size), 0) // HD
    lane_head = lax.broadcasted_iota(jnp.int32, (size, size), 1) // HD
    square = jnp.zeros((8, rows), jnp.float32)
    for g in range(steps):
        part = pl.ds(g * size, size)
        small = (own_ref[g] + prior_ref[g]).astype(jnp.bfloat16)
        tall = jnp.concatenate([small] * (size // HD), axis=0)
        weights = jnp.where(row_head == lane_head, tall, jnp.zeros_like(tall))
        raw = jnp.dot(
            weights, jnp.maximum(q_ref[part, :], 0), preferred_element_type=jnp.float32
        )
        raw_ref[part, :] = raw
        square = square + jnp.sum((raw * raw).reshape(size // 8, 8, rows), axis=0)
    total = jnp.sum(square, axis=0, keepdims=True)
    scale = lax.rsqrt(total * (1.0 / width) + 1e-05)
    for g in range(steps):
        part = pl.ds(g * size, size)
        o_ref[part, :] = (raw_ref[part, :] * scale * gain_ref[part, :]).astype(o_ref.dtype)


def self_mix(queries, own, prior, gain):
    width, rows = queries.shape
    return pl.pallas_call(
        mix_kernel,
        out_shape=jax.ShapeDtypeStruct((width, rows), jnp.bfloat16),
        scratch_shapes=[pltpu.VMEM((width, rows), jnp.float32)],
        compiler_params=pltpu.CompilerParams(vmem_limit_bytes=VMEM_BYTES),
    )(queries, own, prior, gain[:, None])


def attend_kernel(
    slots, tile_rows, tiles, least,
    seen_ref, list_ref, count_ref,
    q_ref, ck_ref, cv_ref, pk_ref, pv_ref, nk_ref, nv_ref, o_ref, k_buf, v_buf,
):
    size = q_ref.shape[0]
    pairs = size // PAIR
    sources = [(ck_ref, cv_ref), (pk_ref, pv_ref)]
    sources += [(nk_ref.at[r], nv_ref.at[r]) for r in range(SPAN - 1)]
    for b, (keys, values) in enumerate(sources):
        for p in range(pairs):
            k_buf[b, p] = keys[pl.ds(p * PAIR, PAIR), :].T
        v_buf[b] = values[...]
    factor = HD ** (-0.5) * math.log2(math.e)
    row = lax.broadcasted_iota(jnp.int32, (slots - least, 2 * tile_rows), 0) + least
    empty = jnp.zeros((HD, tile_rows), jnp.bfloat16)

    def tile(t, blocks):
        columns = pl.ds(pl.multiple_of(t * tile_rows, tile_rows), tile_rows)
        ids = [0] + [list_ref[t * SPAN + i] for i in range(blocks - 1)]
        counts = [None] + [count_ref[ids[i]] for i in range(1, blocks)]
        for p in range(pairs):
            q = q_ref[pl.ds(p * PAIR, PAIR), columns]
            both = jnp.concatenate(
                [
                    jnp.concatenate([q[:HD], empty], axis=1),
                    jnp.concatenate([empty, q[HD:]], axis=1),
                ],
                axis=0,
            )
            scores = []
            peak = None
            for i in range(blocks):
                s = jnp.dot(k_buf[ids[i], p], both, preferred_element_type=jnp.float32)
                if i:
                    s = jnp.concatenate(
                        [s[:least], jnp.where(row < counts[i], s[least:], NEG)], axis=0
                    )
                top = jnp.max(s.reshape(slots // 8, 8, 2 * tile_rows), axis=0)
                peak = top if peak is None else jnp.maximum(peak, top)
                scores.append(s)
            peak = jnp.max(peak, axis=0, keepdims=True)
            denom = None
            acc = None
            for i in range(blocks):
                e = jnp.exp2((scores[i] - peak) * factor)
                part = jnp.sum(e.reshape(slots // 8, 8, 2 * tile_rows), axis=0)
                denom = part if denom is None else denom + part
                added = jnp.dot(
                    v_buf[ids[i], pl.ds(p * PAIR, PAIR), :], e.astype(jnp.bfloat16),
                    preferred_element_type=jnp.float32,
                )
                acc = added if acc is None else acc + added
            inverse = 1.0 / jnp.sum(denom, axis=0, keepdims=True)
            mixed = jnp.concatenate(
                [
                    acc[:HD, :tile_rows] * inverse[:, :tile_rows],
                    acc[HD:, tile_rows:] * inverse[:, tile_rows:],
                ],
                axis=0,
            )
            o_ref[pl.ds(p * PAIR, PAIR), columns] = mixed.astype(o_ref.dtype)

    @pl.loop(0, tiles)
    def _(t):
        for blocks in range(1, SPAN + 2):
            @pl.when(seen_ref[t] == blocks - 1)
            def _():
                tile(t, blocks)


def cross_mix(queries, caption, prompt, near, seen, order, counts):
    width, rows = queries.shape
    slots = caption[0].shape[1]
    tiles = seen.shape[0]
    steps = head_groups(width)
    size = width // steps
    token = pl.BlockSpec((size, rows), lambda g, *_: (g, 0))
    block = pl.BlockSpec((size, slots), lambda g, *_: (g, 0))
    stack = pl.BlockSpec((SPAN - 1, size, slots), lambda g, *_: (0, g, 0))
    return pl.pallas_call(
        functools.partial(attend_kernel, slots, rows // tiles, tiles, slots * 5 // 8),
        grid_spec=pltpu.PrefetchScalarGridSpec(
            num_scalar_prefetch=3,
            grid=(steps,),
            in_specs=[token, block, block, block, block, stack, stack],
            out_specs=token,
            scratch_shapes=[
                pltpu.VMEM((SPAN + 1, size // PAIR, slots, PAIR), jnp.bfloat16),
                pltpu.VMEM((SPAN + 1, size, slots), jnp.bfloat16),
            ],
        ),
        out_shape=jax.ShapeDtypeStruct((width, rows), jnp.bfloat16),
        compiler_params=pltpu.CompilerParams(vmem_limit_bytes=VMEM_BYTES),
    )(seen, order, counts, queries, *caption, *prompt, *near)


def tables(stretch, span_start, span_end, prompt_tokens, region_mask):
    reach = jnp.arange(SPAN, dtype=jnp.int32)
    owner = stretch - reach
    row = jnp.maximum(owner, 0)
    covers = (owner >= 0) & (span_start[row] <= stretch) & (stretch < span_end[row])
    flags = (covers[:, None] & (region_mask[row] == 1)).T.astype(jnp.int32)
    seen = jnp.sum(flags, axis=1)
    place = jnp.cumsum(flags, axis=1) - 1
    hit = (place[:, :, None] == reach[None, None, :]) & (flags[:, :, None] == 1)
    order = jnp.sum(jnp.where(hit, reach[None, :, None] + 1, 0), axis=1)
    counts = jnp.concatenate([jnp.zeros((1,), jnp.int32), prompt_tokens[row]])
    return seen, order.reshape(-1), counts


def local(
    queries, keys, values, cross_queries, prompt_keys, prompt_values, caption_keys,
    caption_values, span_start, span_end, prompt_tokens, region_mask, out_gain,
):
    stretch = lax.axis_index("tm")
    devices = lax.axis_size("tm")
    own = stretch_states(keys.T, values.T)
    gathered = lax.all_gather(own.astype(jnp.bfloat16), "tm")
    earlier = jnp.arange(devices) < stretch
    prior = jnp.sum(
        jnp.where(earlier[:, None, None, None], gathered.astype(jnp.float32), 0.0), axis=0
    )
    self_mixed = self_mix(queries.T, own, prior, out_gain)
    prompt = (prompt_keys[0].T, prompt_values[0].T)
    route = [(i - 1, i) for i in range(1, devices)]
    moving = prompt
    blocks = []
    for _ in range(1, SPAN):
        moving = lax.ppermute(moving, "tm", route)
        blocks.append(moving)
    near = tuple(jnp.stack([b[i] for b in blocks], axis=0) for i in range(2))
    seen, order, counts = tables(stretch, span_start, span_end, prompt_tokens, region_mask)
    cross_mixed = cross_mix(
        cross_queries.T, (caption_keys.T, caption_values.T), prompt, near, seen, order, counts
    )
    return (self_mixed.T, cross_mixed.T)


def solution(mesh):
    rows = P(("groups", "tm"), None)
    blocks = P(("groups", "tm"), None, None)
    in_specs = (
        rows, rows, rows, rows, blocks, blocks, P("groups", None), P("groups", None),
        P("groups"), P("groups"), P("groups"), P("groups", None), P(),
    )
    return jax.shard_map(
        local, mesh=mesh, in_specs=in_specs, out_specs=(rows, rows), check_vma=False
    )
```

```python
import functools
import math

import jax
import jax.numpy as jnp
from jax import lax
from jax.experimental import pallas as pl
from jax.experimental.pallas import tpu as pltpu
from jax.sharding import PartitionSpec as P

HD = 32
SPAN = 6
PAIR = 2 * HD
NEG = -1e30
VMEM_BYTES = 56 * 1024 * 1024


def head_groups(width):
    heads = width // HD
    return next(heads // n for n in (10, 14, 8, 6, 4, 2) if heads % n == 0)


def state_kernel(k_ref, v_ref, s_ref):
    size = k_ref.shape[0]
    full = lax.dot_general(
        v_ref[...], jnp.maximum(k_ref[...], 0), (((1,), (1,)), ((), ())),
        preferred_element_type=jnp.float32,
    )
    lane_head = lax.broadcasted_iota(jnp.int32, (HD, size), 1) // HD
    total = full[:HD, :]
    for h in range(1, size // HD):
        total = jnp.where(lane_head == h, full[h * HD : (h + 1) * HD, :], total)
    s_ref[0] = total


def stretch_states(keys, values):
    width, rows = keys.shape
    steps = head_groups(width)
    size = width // steps
    spec = pl.BlockSpec((size, rows), lambda g: (g, 0))
    return pl.pallas_call(
        state_kernel,
        grid=(steps,),
        in_specs=[spec, spec],
        out_specs=pl.BlockSpec((1, HD, size), lambda g: (g, 0, 0)),
        out_shape=jax.ShapeDtypeStruct((steps, HD, size), jnp.float32),
    )(keys, values)


def mix_kernel(q_ref, own_ref, prior_ref, gain_ref, o_ref, raw_ref):
    steps, _, size = own_ref.shape
    rows = q_ref.shape[1]
    width = steps * size
    row_head = lax.broadcasted_iota(jnp.int32, (size, size), 0) // HD
    lane_head = lax.broadcasted_iota(jnp.int32, (size, size), 1) // HD
    square = jnp.zeros((8, rows), jnp.float32)
    for g in range(steps):
        part = pl.ds(g * size, size)
        small = (own_ref[g] + prior_ref[g]).astype(jnp.bfloat16)
        tall = jnp.concatenate([small] * (size // HD), axis=0)
        weights = jnp.where(row_head == lane_head, tall, jnp.zeros_like(tall))
        raw = jnp.dot(
            weights, jnp.maximum(q_ref[part, :], 0), preferred_element_type=jnp.float32
        )
        raw_ref[part, :] = raw
        square = square + jnp.sum((raw * raw).reshape(size // 8, 8, rows), axis=0)
    total = jnp.sum(square, axis=0, keepdims=True)
    scale = lax.rsqrt(total * (1.0 / width) + 1e-05)
    for g in range(steps):
        part = pl.ds(g * size, size)
        o_ref[part, :] = (raw_ref[part, :] * scale * gain_ref[part, :]).astype(o_ref.dtype)


def self_mix(queries, own, prior, gain):
    width, rows = queries.shape
    return pl.pallas_call(
        mix_kernel,
        out_shape=jax.ShapeDtypeStruct((width, rows), jnp.bfloat16),
        scratch_shapes=[pltpu.VMEM((width, rows), jnp.float32)],
        compiler_params=pltpu.CompilerParams(vmem_limit_bytes=VMEM_BYTES),
    )(queries, own, prior, gain[:, None])


def attend_kernel(
    slots, tile_rows, tiles, least,
    seen_ref, list_ref, count_ref,
    q_ref, ck_ref, cv_ref, pk_ref, pv_ref, nk_ref, nv_ref, o_ref, k_buf, v_buf,
):
    size = q_ref.shape[0]
    pairs = size // PAIR
    sources = [(ck_ref, cv_ref), (pk_ref, pv_ref)]
    sources += [(nk_ref.at[r], nv_ref.at[r]) for r in range(SPAN - 1)]
    for b, (keys, values) in enumerate(sources):
        for p in range(pairs):
            k_buf[b, p] = keys[pl.ds(p * PAIR, PAIR), :].T
        v_buf[b] = values[...]
    factor = HD ** (-0.5) * math.log2(math.e)
    row = lax.broadcasted_iota(jnp.int32, (slots - least, 2 * tile_rows), 0) + least
    empty = jnp.zeros((HD, tile_rows), jnp.bfloat16)

    def tile(t, blocks):
        columns = pl.ds(pl.multiple_of(t * tile_rows, tile_rows), tile_rows)
        ids = [0] + [list_ref[t * SPAN + i] for i in range(blocks - 1)]
        counts = [None] + [count_ref[ids[i]] for i in range(1, blocks)]
        for p in range(pairs):
            q = q_ref[pl.ds(p * PAIR, PAIR), columns]
            both = jnp.concatenate(
                [
                    jnp.concatenate([q[:HD], empty], axis=1),
                    jnp.concatenate([empty, q[HD:]], axis=1),
                ],
                axis=0,
            )
            scores = []
            peak = None
            for i in range(blocks):
                s = jnp.dot(k_buf[ids[i], p], both, preferred_element_type=jnp.float32)
                if i:
                    s = jnp.concatenate(
                        [s[:least], jnp.where(row < counts[i], s[least:], NEG)], axis=0
                    )
                top = jnp.max(s.reshape(slots // 8, 8, 2 * tile_rows), axis=0)
                peak = top if peak is None else jnp.maximum(peak, top)
                scores.append(s)
            peak = jnp.max(peak, axis=0, keepdims=True)
            denom = None
            acc = None
            for i in range(blocks):
                e = jnp.exp2((scores[i] - peak) * factor)
                part = jnp.sum(e.reshape(slots // 8, 8, 2 * tile_rows), axis=0)
                denom = part if denom is None else denom + part
                added = jnp.dot(
                    v_buf[ids[i], pl.ds(p * PAIR, PAIR), :], e.astype(jnp.bfloat16),
                    preferred_element_type=jnp.float32,
                )
                acc = added if acc is None else acc + added
            inverse = 1.0 / jnp.sum(denom, axis=0, keepdims=True)
            mixed = jnp.concatenate(
                [
                    acc[:HD, :tile_rows] * inverse[:, :tile_rows],
                    acc[HD:, tile_rows:] * inverse[:, tile_rows:],
                ],
                axis=0,
            )
            o_ref[pl.ds(p * PAIR, PAIR), columns] = mixed.astype(o_ref.dtype)

    @pl.loop(0, tiles)
    def _(t):
        for blocks in range(1, SPAN + 2):
            @pl.when(seen_ref[t] == blocks - 1)
            def _():
                tile(t, blocks)


def cross_mix(queries, caption, prompt, near, seen, order, counts):
    width, rows = queries.shape
    slots = caption[0].shape[1]
    tiles = seen.shape[0]
    steps = head_groups(width)
    size = width // steps
    token = pl.BlockSpec((size, rows), lambda g, *_: (g, 0))
    block = pl.BlockSpec((size, slots), lambda g, *_: (g, 0))
    stack = pl.BlockSpec((SPAN - 1, size, slots), lambda g, *_: (0, g, 0))
    return pl.pallas_call(
        functools.partial(attend_kernel, slots, rows // tiles, tiles, slots * 5 // 8),
        grid_spec=pltpu.PrefetchScalarGridSpec(
            num_scalar_prefetch=3,
            grid=(steps,),
            in_specs=[token, block, block, block, block, stack, stack],
            out_specs=token,
            scratch_shapes=[
                pltpu.VMEM((SPAN + 1, size // PAIR, slots, PAIR), jnp.bfloat16),
                pltpu.VMEM((SPAN + 1, size, slots), jnp.bfloat16),
            ],
        ),
        out_shape=jax.ShapeDtypeStruct((width, rows), jnp.bfloat16),
        compiler_params=pltpu.CompilerParams(vmem_limit_bytes=VMEM_BYTES),
    )(seen, order, counts, queries, *caption, *prompt, *near)


PLANE = 4
PARTS = 2


def spread_kernel(devices, pk_ref, pv_ref, nk_ref, nv_ref, send_sem, recv_sem):
    me = lax.axis_index("tm")
    spot = me % PLANE
    odd = spot % 2 == 1
    even = spot % 2 == 0
    front = spot < 2
    back = spot >= 2
    rows = pk_ref.shape[0] // PARTS
    items = 2 * PARTS

    def piece(reach, k):
        own, near = ((pk_ref, nk_ref), (pv_ref, nv_ref))[k % 2]
        part = pl.ds((k // 2) * rows, rows)
        return own.at[part, :] if reach == 0 else near.at[reach - 1, part, :]

    def copy(source, target, reach, line, k):
        return pltpu.make_async_remote_copy(
            src_ref=piece(source, k),
            dst_ref=piece(reach, k),
            send_sem=send_sem.at[line, k],
            recv_sem=recv_sem.at[reach - 1, k],
            device_id={"tm": target},
            device_id_type=pl.DeviceIdType.MESH,
        )

    partner = jnp.where(front, me + 2, me - 2)
    greeted = (
        (partner, None), (me + 1, me + 1 < devices), (me - 1, me >= 1),
        (me + PLANE, me + PLANE < devices), (me - PLANE, me >= PLANE),
    )
    barrier = pltpu.get_barrier_semaphore()
    for target, there in greeted:
        def hello(target=target):
            pl.semaphore_signal(
                barrier, inc=1, device_id={"tm": target}, device_id_type=pl.DeviceIdType.MESH
            )
        hello() if there is None else pl.when(there)(hello)
    peers = 1
    for target, there in greeted[1:]:
        peers = peers + jnp.where(there, 1, 0)
    pl.semaphore_wait(barrier, peers)

    own_lines = (
        (0, me + PLANE, 4, 0, me + PLANE < devices),
        (0, me + 2, 2, 1, front),
        (0, me + 1, 1, 2, even),
    )
    far = me >= PLANE
    far_lines = (
        (4, me - 2, 2, 3, far & back),
        (4, me + 1, 5, 4, far & (me + 1 < devices)),
        (4, me - 1, 3, 5, far & odd),
    )
    mid = me >= 2
    mid_lines = (
        (2, me + 1, 3, 6, mid & even),
        (2, me - 1, 1, 7, mid & odd),
    )

    def start(lines, k):
        for source, target, reach, line, there in lines:
            @pl.when(there)
            def _():
                copy(source, target, reach, line, k).start()

    def arrived(reach, k):
        @pl.when(me >= reach)
        def _():
            copy(reach, partner, reach, 0, k).wait_recv()

    for k in range(items):
        start(own_lines, k)
    for k in range(items + 1):
        if k < items:
            arrived(4, k)
            start(far_lines, k)
        if k >= 1:
            arrived(2, k - 1)
            start(mid_lines, k - 1)
    for k in range(items):
        for reach in (1, 3, 5):
            arrived(reach, k)
    for k in range(items):
        for source, target, reach, line, there in own_lines + far_lines + mid_lines:
            @pl.when(there)
            def _():
                copy(source, target, reach, line, k).wait_send()


def spread(prompt_keys, prompt_values, devices):
    width, slots = prompt_keys.shape
    stack = jax.ShapeDtypeStruct((SPAN - 1, width, slots), prompt_keys.dtype)
    anywhere = pl.BlockSpec(memory_space=pl.ANY)
    return pl.pallas_call(
        functools.partial(spread_kernel, devices),
        out_shape=(stack, stack),
        in_specs=[anywhere, anywhere],
        out_specs=(anywhere, anywhere),
        scratch_shapes=[
            pltpu.SemaphoreType.DMA((8, 2 * PARTS)),
            pltpu.SemaphoreType.DMA((SPAN - 1, 2 * PARTS)),
        ],
        compiler_params=pltpu.CompilerParams(collective_id=0, has_side_effects=True),
    )(prompt_keys, prompt_values)


def tables(stretch, span_start, span_end, prompt_tokens, region_mask):
    reach = jnp.arange(SPAN, dtype=jnp.int32)
    owner = stretch - reach
    row = jnp.maximum(owner, 0)
    covers = (owner >= 0) & (span_start[row] <= stretch) & (stretch < span_end[row])
    flags = (covers[:, None] & (region_mask[row] == 1)).T.astype(jnp.int32)
    seen = jnp.sum(flags, axis=1)
    place = jnp.cumsum(flags, axis=1) - 1
    hit = (place[:, :, None] == reach[None, None, :]) & (flags[:, :, None] == 1)
    order = jnp.sum(jnp.where(hit, reach[None, :, None] + 1, 0), axis=1)
    counts = jnp.concatenate([jnp.zeros((1,), jnp.int32), prompt_tokens[row]])
    return seen, order.reshape(-1), counts


def local(
    queries, keys, values, cross_queries, prompt_keys, prompt_values, caption_keys,
    caption_values, span_start, span_end, prompt_tokens, region_mask, out_gain,
):
    stretch = lax.axis_index("tm")
    devices = lax.axis_size("tm")
    own = stretch_states(keys.T, values.T)
    gathered = lax.all_gather(own.astype(jnp.bfloat16), "tm")
    earlier = jnp.arange(devices) < stretch
    prior = jnp.sum(
        jnp.where(earlier[:, None, None, None], gathered.astype(jnp.float32), 0.0), axis=0
    )
    self_mixed = self_mix(queries.T, own, prior, out_gain)
    prompt = (prompt_keys[0].T, prompt_values[0].T)
    near = spread(*prompt, devices)
    seen, order, counts = tables(stretch, span_start, span_end, prompt_tokens, region_mask)
    cross_mixed = cross_mix(
        cross_queries.T, (caption_keys.T, caption_values.T), prompt, near, seen, order, counts
    )
    return (self_mixed.T, cross_mixed.T)


def solution(mesh):
    rows = P(("groups", "tm"), None)
    blocks = P(("groups", "tm"), None, None)
    in_specs = (
        rows, rows, rows, rows, blocks, blocks, P("groups", None), P("groups", None),
        P("groups"), P("groups"), P("groups"), P("groups", None), P(),
    )
    return jax.shard_map(
        local, mesh=mesh, in_specs=in_specs, out_specs=(rows, rows), check_vma=False
    )
```

```python
import functools
import math

import jax
import jax.numpy as jnp
from jax import lax
from jax.experimental import pallas as pl
from jax.experimental.pallas import tpu as pltpu
from jax.sharding import PartitionSpec as P

HD = 32
SPAN = 6
PAIR = 2 * HD
NEG = -1e30
VMEM_BYTES = 56 * 1024 * 1024


def head_groups(width):
    heads = width // HD
    return next(heads // n for n in (10, 14, 8, 6, 4, 2) if heads % n == 0)


def state_part(keys, values):
    size = keys.shape[0]
    full = lax.dot_general(
        values, jnp.maximum(keys, 0), (((1,), (1,)), ((), ())),
        preferred_element_type=jnp.float32,
    )
    lane_head = lax.broadcasted_iota(jnp.int32, (HD, size), 1) // HD
    total = full[:HD, :]
    for h in range(1, size // HD):
        total = jnp.where(lane_head == h, full[h * HD : (h + 1) * HD, :], total)
    return total


def mix_kernel(q_ref, own_ref, prior_ref, gain_ref, o_ref, raw_ref):
    steps, _, size = own_ref.shape
    rows = q_ref.shape[1]
    width = steps * size
    row_head = lax.broadcasted_iota(jnp.int32, (size, size), 0) // HD
    lane_head = lax.broadcasted_iota(jnp.int32, (size, size), 1) // HD
    square = jnp.zeros((8, rows), jnp.float32)
    for g in range(steps):
        part = pl.ds(g * size, size)
        small = (own_ref[g] + prior_ref[g]).astype(jnp.bfloat16)
        tall = jnp.concatenate([small] * (size // HD), axis=0)
        weights = jnp.where(row_head == lane_head, tall, jnp.zeros_like(tall))
        raw = jnp.dot(
            weights, jnp.maximum(q_ref[part, :], 0), preferred_element_type=jnp.float32
        )
        raw_ref[part, :] = raw
        square = square + jnp.sum((raw * raw).reshape(size // 8, 8, rows), axis=0)
    total = jnp.sum(square, axis=0, keepdims=True)
    scale = lax.rsqrt(total * (1.0 / width) + 1e-05)
    for g in range(steps):
        part = pl.ds(g * size, size)
        o_ref[part, :] = (raw_ref[part, :] * scale * gain_ref[part, :]).astype(o_ref.dtype)


def self_mix(queries, own, prior, gain):
    width, rows = queries.shape
    return pl.pallas_call(
        mix_kernel,
        out_shape=jax.ShapeDtypeStruct((width, rows), jnp.bfloat16),
        scratch_shapes=[pltpu.VMEM((width, rows), jnp.float32)],
        compiler_params=pltpu.CompilerParams(vmem_limit_bytes=VMEM_BYTES),
    )(queries, own, prior, gain[:, None])


def attend_kernel(
    slots, tile_rows, tiles, least,
    seen_ref, list_ref, count_ref,
    q_ref, ck_ref, cv_ref, pk_ref, pv_ref, nk_ref, nv_ref, o_ref, k_buf, v_buf,
):
    size = q_ref.shape[0]
    pairs = size // PAIR
    sources = [(ck_ref, cv_ref), (pk_ref, pv_ref)]
    sources += [(nk_ref.at[r], nv_ref.at[r]) for r in range(SPAN - 1)]
    for b, (keys, values) in enumerate(sources):
        for p in range(pairs):
            k_buf[b, p] = keys[pl.ds(p * PAIR, PAIR), :].T
        v_buf[b] = values[...]
    factor = HD ** (-0.5) * math.log2(math.e)
    row = lax.broadcasted_iota(jnp.int32, (slots - least, 2 * tile_rows), 0) + least
    empty = jnp.zeros((HD, tile_rows), jnp.bfloat16)

    def tile(t, blocks):
        columns = pl.ds(pl.multiple_of(t * tile_rows, tile_rows), tile_rows)
        ids = [0] + [list_ref[t * SPAN + i] for i in range(blocks - 1)]
        counts = [None] + [count_ref[ids[i]] for i in range(1, blocks)]
        for p in range(pairs):
            q = q_ref[pl.ds(p * PAIR, PAIR), columns]
            both = jnp.concatenate(
                [
                    jnp.concatenate([q[:HD], empty], axis=1),
                    jnp.concatenate([empty, q[HD:]], axis=1),
                ],
                axis=0,
            )
            scores = []
            peak = None
            for i in range(blocks):
                s = jnp.dot(k_buf[ids[i], p], both, preferred_element_type=jnp.float32)
                if i:
                    s = jnp.concatenate(
                        [s[:least], jnp.where(row < counts[i], s[least:], NEG)], axis=0
                    )
                top = jnp.max(s.reshape(slots // 8, 8, 2 * tile_rows), axis=0)
                peak = top if peak is None else jnp.maximum(peak, top)
                scores.append(s)
            peak = jnp.max(peak, axis=0, keepdims=True)
            denom = None
            acc = None
            for i in range(blocks):
                e = jnp.exp2((scores[i] - peak) * factor)
                part = jnp.sum(e.reshape(slots // 8, 8, 2 * tile_rows), axis=0)
                denom = part if denom is None else denom + part
                added = jnp.dot(
                    v_buf[ids[i], pl.ds(p * PAIR, PAIR), :], e.astype(jnp.bfloat16),
                    preferred_element_type=jnp.float32,
                )
                acc = added if acc is None else acc + added
            inverse = 1.0 / jnp.sum(denom, axis=0, keepdims=True)
            mixed = jnp.concatenate(
                [
                    acc[:HD, :tile_rows] * inverse[:, :tile_rows],
                    acc[HD:, tile_rows:] * inverse[:, tile_rows:],
                ],
                axis=0,
            )
            o_ref[pl.ds(p * PAIR, PAIR), columns] = mixed.astype(o_ref.dtype)

    @pl.loop(0, tiles)
    def _(t):
        for blocks in range(1, SPAN + 2):
            @pl.when(seen_ref[t] == blocks - 1)
            def _():
                tile(t, blocks)


def cross_mix(queries, caption, prompt, near, seen, order, counts):
    width, rows = queries.shape
    slots = caption[0].shape[1]
    tiles = seen.shape[0]
    steps = head_groups(width)
    size = width // steps
    token = pl.BlockSpec((size, rows), lambda g, *_: (g, 0))
    block = pl.BlockSpec((size, slots), lambda g, *_: (g, 0))
    stack = pl.BlockSpec((SPAN - 1, size, slots), lambda g, *_: (0, g, 0))
    return pl.pallas_call(
        functools.partial(attend_kernel, slots, rows // tiles, tiles, slots * 5 // 8),
        grid_spec=pltpu.PrefetchScalarGridSpec(
            num_scalar_prefetch=3,
            grid=(steps,),
            in_specs=[token, block, block, block, block, stack, stack],
            out_specs=token,
            scratch_shapes=[
                pltpu.VMEM((SPAN + 1, size // PAIR, slots, PAIR), jnp.bfloat16),
                pltpu.VMEM((SPAN + 1, size, slots), jnp.bfloat16),
            ],
        ),
        out_shape=jax.ShapeDtypeStruct((width, rows), jnp.bfloat16),
        compiler_params=pltpu.CompilerParams(vmem_limit_bytes=VMEM_BYTES),
    )(seen, order, counts, queries, *caption, *prompt, *near)


PLANE = 4
PARTS = 2


def spread_kernel(
    devices, pk_ref, pv_ref, k_ref, v_ref, nk_ref, nv_ref, own_ref, sent_ref, send_sem, recv_sem
):
    me = lax.axis_index("tm")
    spot = me % PLANE
    odd = spot % 2 == 1
    even = spot % 2 == 0
    front = spot < 2
    back = spot >= 2
    rows = pk_ref.shape[0] // PARTS
    items = 2 * PARTS

    def piece(reach, k):
        own, near = ((pk_ref, nk_ref), (pv_ref, nv_ref))[k % 2]
        part = pl.ds((k // 2) * rows, rows)
        return own.at[part, :] if reach == 0 else near.at[reach - 1, part, :]

    def copy(source, target, reach, line, k):
        return pltpu.make_async_remote_copy(
            src_ref=piece(source, k),
            dst_ref=piece(reach, k),
            send_sem=send_sem.at[line, k],
            recv_sem=recv_sem.at[reach - 1, k],
            device_id={"tm": target},
            device_id_type=pl.DeviceIdType.MESH,
        )

    partner = jnp.where(front, me + 2, me - 2)
    greeted = (
        (partner, None), (me + 1, me + 1 < devices), (me - 1, me >= 1),
        (me + PLANE, me + PLANE < devices), (me - PLANE, me >= PLANE),
    )
    barrier = pltpu.get_barrier_semaphore()
    for target, there in greeted:
        def hello(target=target):
            pl.semaphore_signal(
                barrier, inc=1, device_id={"tm": target}, device_id_type=pl.DeviceIdType.MESH
            )
        hello() if there is None else pl.when(there)(hello)
    peers = 1
    for target, there in greeted[1:]:
        peers = peers + jnp.where(there, 1, 0)
    pl.semaphore_wait(barrier, peers)

    own_lines = (
        (0, me + PLANE, 4, 0, me + PLANE < devices),
        (0, me + 2, 2, 1, front),
        (0, me + 1, 1, 2, even),
    )
    far = me >= PLANE
    far_lines = (
        (4, me - 2, 2, 3, far & back),
        (4, me + 1, 5, 4, far & (me + 1 < devices)),
        (4, me - 1, 3, 5, far & odd),
    )
    mid = me >= 2
    mid_lines = (
        (2, me + 1, 3, 6, mid & even),
        (2, me - 1, 1, 7, mid & odd),
    )

    def start(lines, k):
        for source, target, reach, line, there in lines:
            @pl.when(there)
            def _():
                copy(source, target, reach, line, k).start()

    def arrived(reach, k):
        @pl.when(me >= reach)
        def _():
            copy(reach, partner, reach, 0, k).wait_recv()

    for k in range(items):
        start(own_lines, k)
    size = own_ref.shape[2]
    for g in range(own_ref.shape[0]):
        part = pl.ds(g * size, size)
        state = state_part(k_ref[part, :], v_ref[part, :])
        own_ref[g] = state
        sent_ref[g] = state.astype(jnp.bfloat16)
    for k in range(items + 1):
        if k < items:
            arrived(4, k)
            start(far_lines, k)
        if k >= 1:
            arrived(2, k - 1)
            start(mid_lines, k - 1)
    for k in range(items):
        for reach in (1, 3, 5):
            arrived(reach, k)
    for k in range(items):
        for source, target, reach, line, there in own_lines + far_lines + mid_lines:
            @pl.when(there)
            def _():
                copy(source, target, reach, line, k).wait_send()


def spread(prompt_keys, prompt_values, keys, values, devices):
    width, slots = prompt_keys.shape
    stack = jax.ShapeDtypeStruct((SPAN - 1, width, slots), prompt_keys.dtype)
    steps = head_groups(width)
    state = (steps, HD, width // steps)
    anywhere = pl.BlockSpec(memory_space=pl.ANY)
    whole = pl.BlockSpec(memory_space=pltpu.VMEM)
    return pl.pallas_call(
        functools.partial(spread_kernel, devices),
        out_shape=(
            stack, stack, jax.ShapeDtypeStruct(state, jnp.float32),
            jax.ShapeDtypeStruct(state, jnp.bfloat16),
        ),
        in_specs=[anywhere, anywhere, whole, whole],
        out_specs=(anywhere, anywhere, whole, whole),
        scratch_shapes=[
            pltpu.SemaphoreType.DMA((8, 2 * PARTS)),
            pltpu.SemaphoreType.DMA((SPAN - 1, 2 * PARTS)),
        ],
        compiler_params=pltpu.CompilerParams(
            collective_id=0, has_side_effects=True, vmem_limit_bytes=VMEM_BYTES
        ),
    )(prompt_keys, prompt_values, keys, values)


def tables(stretch, span_start, span_end, prompt_tokens, region_mask):
    reach = jnp.arange(SPAN, dtype=jnp.int32)
    owner = stretch - reach
    row = jnp.maximum(owner, 0)
    covers = (owner >= 0) & (span_start[row] <= stretch) & (stretch < span_end[row])
    flags = (covers[:, None] & (region_mask[row] == 1)).T.astype(jnp.int32)
    seen = jnp.sum(flags, axis=1)
    place = jnp.cumsum(flags, axis=1) - 1
    hit = (place[:, :, None] == reach[None, None, :]) & (flags[:, :, None] == 1)
    order = jnp.sum(jnp.where(hit, reach[None, :, None] + 1, 0), axis=1)
    counts = jnp.concatenate([jnp.zeros((1,), jnp.int32), prompt_tokens[row]])
    return seen, order.reshape(-1), counts


def local(
    queries, keys, values, cross_queries, prompt_keys, prompt_values, caption_keys,
    caption_values, span_start, span_end, prompt_tokens, region_mask, out_gain,
):
    stretch = lax.axis_index("tm")
    devices = lax.axis_size("tm")
    prompt = (prompt_keys[0].T, prompt_values[0].T)
    *near, own, sent = spread(*prompt, keys.T, values.T, devices)
    gathered = lax.all_gather(sent, "tm")
    earlier = jnp.arange(devices) < stretch
    prior = jnp.sum(
        jnp.where(earlier[:, None, None, None], gathered.astype(jnp.float32), 0.0), axis=0
    )
    self_mixed = self_mix(queries.T, own, prior, out_gain)
    seen, order, counts = tables(stretch, span_start, span_end, prompt_tokens, region_mask)
    cross_mixed = cross_mix(
        cross_queries.T, (caption_keys.T, caption_values.T), prompt, near, seen, order, counts
    )
    return (self_mixed.T, cross_mixed.T)


def solution(mesh):
    rows = P(("groups", "tm"), None)
    blocks = P(("groups", "tm"), None, None)
    in_specs = (
        rows, rows, rows, rows, blocks, blocks, P("groups", None), P("groups", None),
        P("groups"), P("groups"), P("groups"), P("groups", None), P(),
    )
    return jax.shard_map(
        local, mesh=mesh, in_specs=in_specs, out_specs=(rows, rows), check_vma=False
    )
```

```python
import functools
import math

import jax
import jax.numpy as jnp
from jax import lax
from jax.experimental import pallas as pl
from jax.experimental.pallas import tpu as pltpu
from jax.sharding import PartitionSpec as P

HD = 32
SPAN = 6
PAIR = 2 * HD
NEG = -1e30
VMEM_BYTES = 56 * 1024 * 1024


def head_groups(width):
    heads = width // HD
    return next(heads // n for n in (10, 14, 8, 6, 4, 2) if heads % n == 0)


def state_part(keys, values):
    size = keys.shape[0]
    full = lax.dot_general(
        values, jnp.maximum(keys, 0), (((1,), (1,)), ((), ())),
        preferred_element_type=jnp.float32,
    )
    lane_head = lax.broadcasted_iota(jnp.int32, (HD, size), 1) // HD
    total = full[:HD, :]
    for h in range(1, size // HD):
        total = jnp.where(lane_head == h, full[h * HD : (h + 1) * HD, :], total)
    return total


def mix_kernel(q_ref, own_ref, prior_ref, gain_ref, o_ref, raw_ref):
    steps, _, size = own_ref.shape
    rows = q_ref.shape[1]
    width = steps * size
    row_head = lax.broadcasted_iota(jnp.int32, (size, size), 0) // HD
    lane_head = lax.broadcasted_iota(jnp.int32, (size, size), 1) // HD
    square = jnp.zeros((8, rows), jnp.float32)
    for g in range(steps):
        part = pl.ds(g * size, size)
        small = (own_ref[g] + prior_ref[g]).astype(jnp.bfloat16)
        tall = jnp.concatenate([small] * (size // HD), axis=0)
        weights = jnp.where(row_head == lane_head, tall, jnp.zeros_like(tall))
        raw = jnp.dot(
            weights, jnp.maximum(q_ref[part, :], 0), preferred_element_type=jnp.float32
        )
        raw_ref[part, :] = raw
        square = square + jnp.sum((raw * raw).reshape(size // 8, 8, rows), axis=0)
    total = jnp.sum(square, axis=0, keepdims=True)
    scale = lax.rsqrt(total * (1.0 / width) + 1e-05)
    for g in range(steps):
        part = pl.ds(g * size, size)
        o_ref[part, :] = (raw_ref[part, :] * scale * gain_ref[part, :]).astype(o_ref.dtype)


def self_mix(queries, own, prior, gain):
    width, rows = queries.shape
    return pl.pallas_call(
        mix_kernel,
        out_shape=jax.ShapeDtypeStruct((width, rows), jnp.bfloat16),
        scratch_shapes=[pltpu.VMEM((width, rows), jnp.float32)],
        compiler_params=pltpu.CompilerParams(vmem_limit_bytes=VMEM_BYTES),
    )(queries, own, prior, gain[:, None])


def attend_kernel(
    slots, tile_rows, tiles, least,
    seen_ref, list_ref, count_ref,
    q_ref, ck_ref, cv_ref, pk_ref, pv_ref, nk_ref, nv_ref, o_ref, k_buf, v_buf,
):
    size = q_ref.shape[0]
    pairs = size // PAIR
    sources = [(ck_ref, cv_ref), (pk_ref, pv_ref)]
    sources += [(nk_ref.at[r], nv_ref.at[r]) for r in range(SPAN - 1)]
    for b, (keys, values) in enumerate(sources):
        def fill(b=b, keys=keys, values=values):
            for p in range(pairs):
                k_buf[b, p] = keys[pl.ds(p * PAIR, PAIR), :].T
            v_buf[b] = values[...]
        fill() if b == 0 else pl.when(count_ref[b] > 0)(fill)
    factor = HD ** (-0.5) * math.log2(math.e)
    row = lax.broadcasted_iota(jnp.int32, (slots - least, 2 * tile_rows), 0) + least
    empty = jnp.zeros((HD, tile_rows), jnp.bfloat16)

    def tile(t, blocks):
        columns = pl.ds(pl.multiple_of(t * tile_rows, tile_rows), tile_rows)
        ids = [0] + [list_ref[t * SPAN + i] for i in range(blocks - 1)]
        counts = [None] + [count_ref[ids[i]] for i in range(1, blocks)]
        for p in range(pairs):
            q = q_ref[pl.ds(p * PAIR, PAIR), columns]
            both = jnp.concatenate(
                [
                    jnp.concatenate([q[:HD], empty], axis=1),
                    jnp.concatenate([empty, q[HD:]], axis=1),
                ],
                axis=0,
            )
            scores = []
            peak = None
            for i in range(blocks):
                s = jnp.dot(k_buf[ids[i], p], both, preferred_element_type=jnp.float32)
                if i:
                    s = jnp.concatenate(
                        [s[:least], jnp.where(row < counts[i], s[least:], NEG)], axis=0
                    )
                top = jnp.max(s.reshape(slots // 8, 8, 2 * tile_rows), axis=0)
                peak = top if peak is None else jnp.maximum(peak, top)
                scores.append(s)
            peak = jnp.max(peak, axis=0, keepdims=True)
            denom = None
            acc = None
            for i in range(blocks):
                e = jnp.exp2((scores[i] - peak) * factor)
                part = jnp.sum(e.reshape(slots // 8, 8, 2 * tile_rows), axis=0)
                denom = part if denom is None else denom + part
                added = jnp.dot(
                    v_buf[ids[i], pl.ds(p * PAIR, PAIR), :], e.astype(jnp.bfloat16),
                    preferred_element_type=jnp.float32,
                )
                acc = added if acc is None else acc + added
            inverse = 1.0 / jnp.sum(denom, axis=0, keepdims=True)
            mixed = jnp.concatenate(
                [
                    acc[:HD, :tile_rows] * inverse[:, :tile_rows],
                    acc[HD:, tile_rows:] * inverse[:, tile_rows:],
                ],
                axis=0,
            )
            o_ref[pl.ds(p * PAIR, PAIR), columns] = mixed.astype(o_ref.dtype)

    @pl.loop(0, tiles)
    def _(t):
        for blocks in range(1, SPAN + 2):
            @pl.when(seen_ref[t] == blocks - 1)
            def _():
                tile(t, blocks)


def cross_mix(queries, caption, prompt, near, seen, order, counts):
    width, rows = queries.shape
    slots = caption[0].shape[1]
    tiles = seen.shape[0]
    steps = head_groups(width)
    size = width // steps
    token = pl.BlockSpec((size, rows), lambda g, *_: (g, 0))
    block = pl.BlockSpec((size, slots), lambda g, *_: (g, 0))
    stack = pl.BlockSpec((SPAN - 1, size, slots), lambda g, *_: (0, g, 0))
    return pl.pallas_call(
        functools.partial(attend_kernel, slots, rows // tiles, tiles, slots * 5 // 8),
        grid_spec=pltpu.PrefetchScalarGridSpec(
            num_scalar_prefetch=3,
            grid=(steps,),
            in_specs=[token, block, block, block, block, stack, stack],
            out_specs=token,
            scratch_shapes=[
                pltpu.VMEM((SPAN + 1, size // PAIR, slots, PAIR), jnp.bfloat16),
                pltpu.VMEM((SPAN + 1, size, slots), jnp.bfloat16),
            ],
        ),
        out_shape=jax.ShapeDtypeStruct((width, rows), jnp.bfloat16),
        compiler_params=pltpu.CompilerParams(vmem_limit_bytes=VMEM_BYTES),
    )(seen, order, counts, queries, *caption, *prompt, *near)


PLANE = 4
PARTS = 2


def spread_kernel(
    devices, pk_ref, pv_ref, k_ref, v_ref, nk_ref, nv_ref, own_ref, sent_ref, send_sem, recv_sem
):
    me = lax.axis_index("tm")
    spot = me % PLANE
    odd = spot % 2 == 1
    even = spot % 2 == 0
    front = spot < 2
    back = spot >= 2
    rows = pk_ref.shape[0] // PARTS
    items = 2 * PARTS

    def piece(reach, k):
        own, near = ((pk_ref, nk_ref), (pv_ref, nv_ref))[k % 2]
        part = pl.ds((k // 2) * rows, rows)
        return own.at[part, :] if reach == 0 else near.at[reach - 1, part, :]

    def copy(source, target, reach, line, k):
        return pltpu.make_async_remote_copy(
            src_ref=piece(source, k),
            dst_ref=piece(reach, k),
            send_sem=send_sem.at[line, k],
            recv_sem=recv_sem.at[reach - 1, k],
            device_id={"tm": target},
            device_id_type=pl.DeviceIdType.MESH,
        )

    partner = jnp.where(front, me + 2, me - 2)
    greeted = (
        (partner, None), (me + 1, me + 1 < devices), (me - 1, me >= 1),
        (me + PLANE, me + PLANE < devices), (me - PLANE, me >= PLANE),
    )
    barrier = pltpu.get_barrier_semaphore()
    for target, there in greeted:
        def hello(target=target):
            pl.semaphore_signal(
                barrier, inc=1, device_id={"tm": target}, device_id_type=pl.DeviceIdType.MESH
            )
        hello() if there is None else pl.when(there)(hello)
    peers = 1
    for target, there in greeted[1:]:
        peers = peers + jnp.where(there, 1, 0)
    pl.semaphore_wait(barrier, peers)

    own_lines = (
        (0, me + PLANE, 4, 0, me + PLANE < devices),
        (0, me + 2, 2, 1, front),
        (0, me + 1, 1, 2, even),
    )
    far = me >= PLANE
    far_lines = (
        (4, me - 2, 2, 3, far & back),
        (4, me + 1, 5, 4, far & (me + 1 < devices)),
        (4, me - 1, 3, 5, far & odd),
    )
    mid = me >= 2
    mid_lines = (
        (2, me + 1, 3, 6, mid & even),
        (2, me - 1, 1, 7, mid & odd),
    )

    def start(lines, k):
        for source, target, reach, line, there in lines:
            @pl.when(there)
            def _():
                copy(source, target, reach, line, k).start()

    def arrived(reach, k):
        @pl.when(me >= reach)
        def _():
            copy(reach, partner, reach, 0, k).wait_recv()

    for k in range(items):
        start(own_lines, k)
    size = own_ref.shape[2]
    for g in range(own_ref.shape[0]):
        part = pl.ds(g * size, size)
        state = state_part(k_ref[part, :], v_ref[part, :])
        own_ref[g] = state
        sent_ref[g] = state.astype(jnp.bfloat16)
    for k in range(items + 1):
        if k < items:
            arrived(4, k)
            start(far_lines, k)
        if k >= 1:
            arrived(2, k - 1)
            start(mid_lines, k - 1)
    for k in range(items):
        for reach in (1, 3, 5):
            arrived(reach, k)
    for k in range(items):
        for source, target, reach, line, there in own_lines + far_lines + mid_lines:
            @pl.when(there)
            def _():
                copy(source, target, reach, line, k).wait_send()


def spread(prompt_keys, prompt_values, keys, values, devices):
    width, slots = prompt_keys.shape
    stack = jax.ShapeDtypeStruct((SPAN - 1, width, slots), prompt_keys.dtype)
    steps = head_groups(width)
    state = (steps, HD, width // steps)
    anywhere = pl.BlockSpec(memory_space=pl.ANY)
    whole = pl.BlockSpec(memory_space=pltpu.VMEM)
    return pl.pallas_call(
        functools.partial(spread_kernel, devices),
        out_shape=(
            stack, stack, jax.ShapeDtypeStruct(state, jnp.float32),
            jax.ShapeDtypeStruct(state, jnp.bfloat16),
        ),
        in_specs=[anywhere, anywhere, whole, whole],
        out_specs=(anywhere, anywhere, whole, whole),
        scratch_shapes=[
            pltpu.SemaphoreType.DMA((8, 2 * PARTS)),
            pltpu.SemaphoreType.DMA((SPAN - 1, 2 * PARTS)),
        ],
        compiler_params=pltpu.CompilerParams(
            collective_id=0, has_side_effects=True, vmem_limit_bytes=VMEM_BYTES
        ),
    )(prompt_keys, prompt_values, keys, values)


def tables(stretch, span_start, span_end, prompt_tokens, region_mask):
    reach = jnp.arange(SPAN, dtype=jnp.int32)
    owner = stretch - reach
    row = jnp.maximum(owner, 0)
    covers = (owner >= 0) & (span_start[row] <= stretch) & (stretch < span_end[row])
    flags = (covers[:, None] & (region_mask[row] == 1)).T.astype(jnp.int32)
    seen = jnp.sum(flags, axis=1)
    place = jnp.cumsum(flags, axis=1) - 1
    hit = (place[:, :, None] == reach[None, None, :]) & (flags[:, :, None] == 1)
    order = jnp.sum(jnp.where(hit, reach[None, :, None] + 1, 0), axis=1)
    counts = jnp.concatenate(
        [jnp.zeros((1,), jnp.int32), jnp.where(flags.sum(axis=0) > 0, prompt_tokens[row], 0)]
    )
    return seen, order.reshape(-1), counts


def local(
    queries, keys, values, cross_queries, prompt_keys, prompt_values, caption_keys,
    caption_values, span_start, span_end, prompt_tokens, region_mask, out_gain,
):
    stretch = lax.axis_index("tm")
    devices = lax.axis_size("tm")
    prompt = (prompt_keys[0].T, prompt_values[0].T)
    *near, own, sent = spread(*prompt, keys.T, values.T, devices)
    gathered = lax.all_gather(sent, "tm")
    earlier = jnp.arange(devices) < stretch
    prior = jnp.sum(
        jnp.where(earlier[:, None, None, None], gathered.astype(jnp.float32), 0.0), axis=0
    )
    self_mixed = self_mix(queries.T, own, prior, out_gain)
    seen, order, counts = tables(stretch, span_start, span_end, prompt_tokens, region_mask)
    cross_mixed = cross_mix(
        cross_queries.T, (caption_keys.T, caption_values.T), prompt, near, seen, order, counts
    )
    return (self_mixed.T, cross_mixed.T)


def solution(mesh):
    rows = P(("groups", "tm"), None)
    blocks = P(("groups", "tm"), None, None)
    in_specs = (
        rows, rows, rows, rows, blocks, blocks, P("groups", None), P("groups", None),
        P("groups"), P("groups"), P("groups"), P("groups", None), P(),
    )
    return jax.shard_map(
        local, mesh=mesh, in_specs=in_specs, out_specs=(rows, rows), check_vma=False
    )
```
